32 devices in a mesh: groups: 2 (over x), seq: 16 (over z, y, core).
Axes of the slice: x: 2, y: 2, z: 4, core: 2. Of those that a mesh axis runs over, the one named last changes fastest.
Arguments:
- queries: bfloat16 [4096, 2048], P(('groups', 'seq')), parts along dimension 0, may hold values from -2.5 to 2.5
- keys: bfloat16 [4096, 2048], P(('groups', 'seq')), parts along dimension 0, may hold values from -2.5 to 2.5
- values: bfloat16 [4096, 2048], P(('groups', 'seq')), parts along dimension 0, may hold values from -6 to 6
- grad_out: bfloat16 [4096, 2048], P(('groups', 'seq')), parts along dimension 0, may hold values from -6 to 6
- doc_lengths: int32 [16], P('groups'), parts along dimension 0, may hold values from 1 to 896, 2048 in all
Outputs:
- attn_out: bfloat16 [4096, 2048], P(('groups', 'seq')), parts along dimension 0
- grad_queries: bfloat16 [4096, 2048], P(('groups', 'seq')), parts along dimension 0
- grad_keys: bfloat16 [4096, 2048], P(('groups', 'seq')), parts along dimension 0
- grad_values: bfloat16 [4096, 2048], P(('groups', 'seq')), parts along dimension 0
The draws below stay inside these ranges and needn't reach their ends.
There are 2 independent parts, one for each index of `groups`. The reference program is written for one: setup_inputs(seed, part) draws one part's arguments, and reference() takes and returns one part's arrays. A program takes and returns all parts, laid end to end along the dimension named above; each array names one. Nothing has to cross between parts.
Inputs may be any that keep to these rules, and one draw needn't show every extreme that they name: `doc_lengths`: lengths of the documents in order; they sum to 2048 and the longest has exactly 896 tokens.
All inputs are finite; a program needn't handle non-finite values.
Results may differ from the reference program's by a relative error of at most 0.0058.
Values may be sent and summed in bfloat16 or wider, within the bound.
A program may use at most 256 MiB of HBM per device.

```python
import math
import jax
import jax.numpy as jnp
import numpy as np
from jax import lax

HEADS = 16
HD = 128
TOK_DEV = 128
SEQ = 2048
DOCS = 8
MOST = 896
N_SEQ = 16


def levels(stream_key, extent, split, low, high):
    loudness, own = 1.0, jax.random.fold_in(stream_key, 6)
    for axis_at, blocks in split:
        steps = jnp.exp(jax.random.uniform(jax.random.fold_in(own, axis_at), (blocks,), jnp.float32, low / len(split), high / len(split)))
        loudness = loudness * jnp.repeat(steps, extent[axis_at] // blocks).reshape([-1 if axis == axis_at else 1 for axis in range(len(extent))])
    return loudness


def split_up(count, total, most, slope):
    loads = [(1 << 20) // math.isqrt(standing ** slope) + 1 for standing in range(2, count + 1)]
    rest, holding = total - most - (count - 1), [1] * (count - 1)
    while rest > 0:
        candidates = [i for i in range(count - 1) if holding[i] < most]
        whole, left = sum([loads[i] for i in candidates]), rest
        for i in candidates:
            extra = min(most - holding[i], max(1, left * loads[i] // whole), rest)
            holding[i] = holding[i] + extra
            rest = rest - extra
    return np.array([most] + holding)


def uneven(own_key, number_of, total, bound, skew):
    if number_of == 2:
        one = jax.random.randint(own_key, (), max(1, total - bound), min(bound, total - 1) + 1)
        return jnp.stack([one, total - one])
    tallies = jnp.asarray(split_up(number_of, total, bound, skew), jnp.int32)
    couples = (number_of - 1) // 2
    donor, sink = tallies[1:1 + 2 * couples:2], tallies[2:2 + 2 * couples:2]
    slack = jnp.minimum(donor - 1, bound - sink)
    moved = jax.random.randint(jax.random.fold_in(own_key, 1), (couples,), 0, 1 << 20) % (slack + 1)
    tallies = tallies.at[1:1 + 2 * couples:2].set(donor - moved).at[2:2 + 2 * couples:2].set(sink + moved)
    return tallies[jax.random.permutation(jax.random.fold_in(own_key, 2), number_of)]


def scatter_about(key, extent, scale, most, pieces=(), kind=jnp.bfloat16):
    result = scale * jax.random.normal(key, extent, jnp.float32)
    if pieces:
        result = result * levels(key, extent, pieces, -0.22, 0.18)
    return jnp.clip(result, -most, most).astype(kind)


def setup_inputs(seed: int = 0, part: int = 0) -> dict:
    arg_keys = jax.random.split(jax.random.key(seed), 6)
    own_keys = jax.random.split(jax.random.fold_in(arg_keys[5], part), 6)
    queries = scatter_about(own_keys[0], (SEQ, HEADS * HD), 0.3, 2.5, ((0, 16),))
    keys = scatter_about(own_keys[1], (SEQ, HEADS * HD), 0.3, 2.5, ((0, 16),))
    values = scatter_about(own_keys[2], (SEQ, HEADS * HD), 1.0, 6.0, ((0, 16),))
    grad_out = scatter_about(own_keys[3], (SEQ, HEADS * HD), 1.0, 6.0, ((0, 16),))
    doc_lengths = uneven(own_keys[4], DOCS, SEQ, MOST, 2).astype(jnp.int32)
    return {"queries": queries, "keys": keys, "values": values, "grad_out": grad_out, "doc_lengths": doc_lengths}


def wide(array):
    return array.astype(jnp.float32)

def reference(queries, keys, values, grad_out, doc_lengths):
    rows_here = TOK_DEV
    block_count = N_SEQ
    seq_total = SEQ
    starts = jnp.cumsum(doc_lengths).astype(jnp.int32) - doc_lengths
    positions = jnp.arange(seq_total, dtype=jnp.int32)
    before = starts[None, :] <= positions[:, None]
    doc_begin = lax.optimization_barrier(jnp.max(jnp.where(before, starts[None, :], 0), axis=1))
    finish = lax.optimization_barrier(jnp.min(jnp.where(before, seq_total, starts[None, :]), axis=1))
    inv_root = 1.0 / jnp.sqrt((positions - doc_begin + 1).astype(jnp.float32))
    query_all = queries.reshape(block_count, rows_here, HEADS, HD)
    key_all = keys.reshape(block_count, rows_here, HEADS, HD)
    value_all = values.reshape(block_count, rows_here, HEADS, HD)
    scaled_all = (wide(grad_out).reshape(seq_total, HEADS, HD) * inv_root[:, None, None]).astype(jnp.bfloat16)
    scaled_all = scaled_all.reshape(block_count, rows_here, HEADS, HD)
    begin_all = doc_begin.reshape(block_count, rows_here)
    finish_all = finish.reshape(block_count, rows_here)
    root_all = inv_root.reshape(block_count, rows_here)
    firsts = jnp.arange(block_count, dtype=jnp.int32) * rows_here
    open_flags = jnp.any((starts[None, :] >= firsts[:, None]) & (starts[None, :] < firsts[:, None] + rows_here), axis=1)
    close_flags = jnp.any((starts[None, :] > firsts[:, None]) & (starts[None, :] <= firsts[:, None] + rows_here), axis=1)

    def block_states(items):
        query_heads, key_heads, value_heads, scaled_grad, begin_rows, finish_rows, first_row = items
        tail_keys = jnp.where((finish_rows >= first_row + rows_here)[:, None, None], key_heads, jnp.zeros((), jnp.bfloat16))
        tail_state = jnp.einsum('shd,she->hde', wide(tail_keys), wide(value_heads))
        head_queries = jnp.where((begin_rows <= first_row)[:, None, None], query_heads, jnp.zeros((), jnp.bfloat16))
        head_state = jnp.einsum('thd,the->hde', wide(head_queries), wide(scaled_grad))
        return (tail_state, head_state)
    tails, heads_all = lax.map(block_states, (query_all, key_all, value_all, scaled_all, begin_all, finish_all, firsts))

    def carry_prefix(running, pair):
        flag_now, tail_state = pair
        return (jnp.where(flag_now, tail_state, running + tail_state), running)
    zero_state = jnp.zeros((HEADS, HD, HD), jnp.float32)
    final_state, carried = lax.scan(carry_prefix, zero_state, (open_flags, tails))
    final_back, returned = lax.scan(carry_prefix, zero_state, (close_flags, heads_all), reverse=True)

    def block_outputs(items):
        query_heads, key_heads, value_heads, scaled_grad, begin_rows, finish_rows, root_rows, first_row, carried_state, returned_state = items
        local_rows = jnp.arange(rows_here, dtype=jnp.int32)
        same_doc = (begin_rows[:, None] == begin_rows[None, :]) & (local_rows[None, :] <= local_rows[:, None])
        use_prefix = (begin_rows < first_row)[:, None, None]
        use_suffix = (finish_rows > first_row + rows_here)[:, None, None]
        carried_low = carried_state.astype(jnp.bfloat16)
        returned_low = returned_state.astype(jnp.bfloat16)
        scores = jnp.einsum('thd,shd->hts', wide(query_heads), wide(key_heads))
        weights = jnp.where(same_doc[None], scores, 0.0).astype(jnp.bfloat16)
        attended = jnp.einsum('hts,she->the', wide(weights), wide(value_heads))
        attended = attended + jnp.where(use_prefix, jnp.einsum('thd,hde->the', wide(query_heads), wide(carried_low)), 0.0)
        attn_rows = (attended * root_rows[:, None, None]).astype(jnp.bfloat16)
        dscores = jnp.einsum('the,she->hts', wide(scaled_grad), wide(value_heads))
        dweights = jnp.where(same_doc[None], dscores, 0.0).astype(jnp.bfloat16)
        grad_query = jnp.einsum('hts,shd->thd', wide(dweights), wide(key_heads))
        grad_query = grad_query + jnp.where(use_prefix, jnp.einsum('the,hde->thd', wide(scaled_grad), wide(carried_low)), 0.0)
        grad_key = jnp.einsum('hts,thd->shd', wide(dweights), wide(query_heads))
        grad_key = grad_key + jnp.where(use_suffix, jnp.einsum('she,hde->shd', wide(value_heads), wide(returned_low)), 0.0)
        grad_value = jnp.einsum('hts,the->she', wide(weights), wide(scaled_grad))
        grad_value = grad_value + jnp.where(use_suffix, jnp.einsum('shd,hde->she', wide(key_heads), wide(returned_low)), 0.0)
        return (attn_rows, grad_query.astype(jnp.bfloat16), grad_key.astype(jnp.bfloat16), grad_value.astype(jnp.bfloat16))
    outputs = lax.map(block_outputs, (query_all, key_all, value_all, scaled_all, begin_all, finish_all, root_all, firsts, carried, returned))
    attn_out = outputs[0].reshape(seq_total, HEADS * HD)
    grad_queries = outputs[1].reshape(seq_total, HEADS * HD)
    grad_keys = outputs[2].reshape(seq_total, HEADS * HD)
    grad_values = outputs[3].reshape(seq_total, HEADS * HD)
    return (attn_out, grad_queries, grad_keys, grad_values)
```

```python
import functools

import jax
import jax.numpy as jnp
from jax import lax
from jax.experimental import pallas as pl
from jax.experimental.pallas import tpu as pltpu
from jax.sharding import PartitionSpec as P

HD = 128
CHUNK = 2
MINOR, ACROSS, NEXT, SECOND, CARRY = range(5)

F32 = jnp.float32
BF16 = jnp.bfloat16


def dot(a, b, contract=(1, 0)):
    dims = (((contract[0],), (contract[1],)), ((), ()))
    return lax.dot_general(a, b, dims, preferred_element_type=F32)


def kernel(n, docs, heads, lengths_hbm, q_hbm, k_hbm, v_hbm, g_hbm, attn_ref, gq_ref, gk_ref, gv_ref,
           lengths, q_ref, k_ref, v_ref, g_ref, load_sems, sg_ref, states, minor_in, sum_out, sum_in, total_out, next_in, second_in, carry_out,
           entering, weights_ref, dweights_ref, send_sems, recv_sems):
    loads = [pltpu.make_async_copy(src, dst, load_sems.at[i]) for i, (src, dst) in enumerate((
        (lengths_hbm, lengths), (g_hbm, g_ref), (q_hbm, q_ref), (k_hbm, k_ref), (v_hbm, v_ref)))]
    for load in loads:
        load.start()
    rows = q_ref.shape[0]
    planes = n // 4
    chunks = heads // CHUNK
    me = lax.axis_index("seq")
    core = lax.rem(me, 2)
    plane = me // 4
    chip = lax.rem(me // 2, 2)
    partner = me + 1 - 2 * core
    across = me + 2 - 4 * chip
    step = 2 * core - 1
    major, minor = 1 - core, core

    def inside(p):
        return (p >= 0) & (p < planes)

    barrier = pltpu.get_barrier_semaphore()

    def greet(device):
        pl.semaphore_signal(barrier, inc=1, device_id={"seq": device},
                            device_id_type=pl.DeviceIdType.MESH)

    greet(partner)
    greet(across)
    for by in (-1, 1):
        @pl.when(inside(plane + by))
        def _():
            greet(me + 4 * by)

    loads[0].wait()
    starts = []
    running = jnp.int32(0)
    for j in range(docs):
        starts.append(running)
        running = running + lengths[j]

    shift = 1 - core

    def clear(first, last):
        lower = first * rows + shift
        upper = (last + 1) * rows + shift
        found = jnp.int32(0)
        for s in starts:
            found = found + jnp.where((s >= lower) & (s < upper), 1, 0)
        return found == 0

    own_clear = clear(me, me)
    partner_clear = clear(partner, partner)
    is_down = chip == core
    down_first = 4 * plane + 2 * core
    up_first = 4 * plane + 2 - 2 * core
    down_clear = clear(down_first, down_first + 1)
    up_clear = clear(up_first, up_first + 1)
    before_first = 4 * (plane - step)
    before_clear = clear(before_first, before_first + 3)
    use_next = inside(plane - step) & (jnp.logical_not(is_down) | up_clear)
    use_second = use_next & before_clear & inside(plane - 2 * step)

    first_row = me * rows
    seq_total = rows * n

    def spans(shape, axis):
        pos = first_row + lax.broadcasted_iota(jnp.int32, shape, axis)
        begin = jnp.zeros(shape, jnp.int32)
        finish = jnp.full(shape, seq_total, jnp.int32)
        for s in starts:
            begin = jnp.where(s <= pos, s, begin)
        for s in reversed(starts):
            finish = jnp.where(s > pos, s, finish)
        return pos, begin, finish

    pos, begin, finish = spans((rows, HD), 0)
    pos_row, begin_row, _ = spans((rows, rows), 1)
    inv_root = 1.0 / jnp.sqrt((pos - begin + 1).astype(F32))
    pos_square, begin_square, _ = spans((rows, rows), 0)
    same_doc = (begin_square == begin_row) & (pos_row <= pos_square)
    tail_rows = jnp.where(finish >= first_row + rows, 1.0, 0.0).astype(BF16)
    head_rows = jnp.where(begin <= first_row, 1.0, 0.0).astype(BF16)
    prefix_rows = jnp.where(begin < first_row, 1.0, 0.0).astype(BF16)
    suffix_rows = jnp.where(finish > first_row + rows, 1.0, 0.0).astype(BF16)

    def columns(h):
        return pl.ds(pl.multiple_of(h * HD, HD), HD)

    def copy(kind, i, src, dst, device):
        return pltpu.make_async_remote_copy(
            src_ref=src, dst_ref=dst, send_sem=send_sems.at[kind, i],
            recv_sem=recv_sems.at[kind, i], device_id={"seq": device},
            device_id_type=pl.DeviceIdType.MESH)

    def part(i):
        return pl.ds(i * CHUNK, CHUNK)

    def minor_copy(i):
        return copy(MINOR, i, states.at[minor, part(i)], minor_in.at[part(i)], partner)

    def across_copy(i):
        return copy(ACROSS, i, sum_out.at[part(i)], sum_in.at[part(i)], across)

    def next_copy(i):
        return copy(NEXT, i, total_out.at[part(i)], next_in.at[part(i)], me + 4 * step)

    def second_copy(i):
        return copy(SECOND, i, next_in.at[part(i)], second_in.at[part(i)], me + 4 * step)

    def carry_copy(i):
        return copy(CARRY, i, carry_out.at[part(i)], entering.at[major, part(i)], partner)

    def own_states(i):
        for j in range(CHUNK):
            h = i * CHUNK + j
            at = columns(h)
            sg = (g_ref[:, at].astype(F32) * inv_root).astype(BF16)
            sg_ref[:, at] = sg
            states[0, h] = dot(k_ref[:, at] * tail_rows, v_ref[:, at], (0, 0)).astype(BF16)
            states[1, h] = dot(q_ref[:, at] * head_rows, sg, (0, 0)).astype(BF16)

    for load in loads[1:]:
        load.wait()
    own_states(0)
    peers = jnp.int32(2)
    for by in (-1, 1):
        peers = peers + jnp.where(inside(plane + by), 1, 0)
    pl.semaphore_wait(barrier, peers)
    minor_copy(0).start()


    def pick(flag, x):
        return jnp.where(flag, x.astype(F32), 0.0)

    def chip_sum(i):
        minor_copy(i).wait_recv()
        for j in range(CHUNK):
            h = i * CHUNK + j
            sum_out[h] = (states[major, h].astype(F32) + pick(own_clear, minor_in[h])).astype(BF16)
        across_copy(i).start()

    @pl.loop(1, chunks + 2)
    def _(i):
        @pl.when(i < chunks)
        def _():
            own_states(i)
            minor_copy(i).start()

        @pl.when(i >= 2)
        def _():
            chip_sum(i - 2)

    def total(i):
        for j in range(CHUNK):
            h = i * CHUNK + j
            at = columns(h)
            scores = dot(q_ref[:, at], k_ref[:, at], (1, 1))
            weights_ref[h] = jnp.where(same_doc, scores, 0.0).astype(BF16)
            dscores = dot(sg_ref[:, at], v_ref[:, at], (1, 1))
            dweights_ref[h] = jnp.where(same_doc, dscores, 0.0).astype(BF16)
        across_copy(i).wait_recv()
        for j in range(CHUNK):
            h = i * CHUNK + j
            total_out[h] = (pick(is_down | down_clear, sum_out[h])
                            + pick(jnp.logical_not(is_down) | down_clear, sum_in[h])).astype(BF16)

        @pl.when(inside(plane + step))
        def _():
            next_copy(i).start()

    relays = inside(plane - step) & inside(plane + step)

    def relay(i):
        @pl.when(inside(plane - step))
        def _():
            next_copy(i).wait_recv()

        @pl.when(relays)
        def _():
            second_copy(i).start()

    def enter(i):
        @pl.when(inside(plane - 2 * step))
        def _():
            second_copy(i).wait_recv()

        for j in range(CHUNK):
            h = i * CHUNK + j
            carry = pick(is_down, sum_in[h]) + pick(use_next, next_in[h]) + pick(use_second, second_in[h])
            carry_out[h] = carry.astype(BF16)
            entering[major, h] = (minor_in[h].astype(F32) + pick(partner_clear, carry)).astype(BF16)
        carry_copy(i).start()

    def finish_heads(i):
        carry_copy(i).wait_recv()
        for j in range(CHUNK):
            h = i * CHUNK + j
            at = columns(h)
            q, k, v, sg = q_ref[:, at], k_ref[:, at], v_ref[:, at], sg_ref[:, at]
            w, dw = weights_ref[h], dweights_ref[h]
            carried, returned = entering[0, h], entering[1, h]
            attended = dot(w, v) + dot(q * prefix_rows, carried)
            attn_ref[:, at] = (attended * inv_root).astype(BF16)
            gq_ref[:, at] = (dot(dw, k) + dot(sg * prefix_rows, carried, (1, 1))).astype(BF16)
            gk_ref[:, at] = (dot(dw, q, (0, 0)) + dot(v * suffix_rows, returned, (1, 1))).astype(BF16)
            gv_ref[:, at] = (dot(w, sg, (0, 0)) + dot(k * suffix_rows, returned)).astype(BF16)

    stages = ((0, total), (2, relay), (4, enter), (5, finish_heads))

    @pl.loop(0, chunks + stages[-1][0])
    def _(i):
        for lag, stage in stages:
            @pl.when((i >= lag) & (i < chunks + lag))
            def _():
                stage(i - lag)

    @pl.loop(0, chunks)
    def _(i):
        minor_copy(i).wait_send()
        across_copy(i).wait_send()
        carry_copy(i).wait_send()

        @pl.when(inside(plane + step))
        def _():
            next_copy(i).wait_send()

        @pl.when(relays)
        def _():
            second_copy(i).wait_send()


def place(*refs):
    sources, targets, sems = refs[:4], refs[4:8], refs[8]
    moves = [pltpu.make_async_copy(src, dst, sems.at[i]) for i, (src, dst) in enumerate(zip(sources, targets))]
    for move in moves:
        move.start()
    for move in moves:
        move.wait()


def per_device(n, queries, keys, values, grad_out, doc_lengths):
    rows, width = queries.shape
    heads = width // HD
    chunks = heads // CHUNK
    remote = pl.BlockSpec(memory_space=pltpu.HBM)
    held = pltpu.VMEM((rows, width), BF16)
    state = pltpu.VMEM((heads, HD, HD), BF16)
    pair = pltpu.VMEM((2, heads, HD, HD), BF16)
    square = pltpu.VMEM((heads, rows, rows), BF16)
    out = jax.ShapeDtypeStruct((rows, width), BF16)
    results = pl.pallas_call(
        functools.partial(kernel, n, doc_lengths.shape[0], heads),
        out_shape=(held,) * 4,
        in_specs=[remote] * 5,
        out_specs=(pl.BlockSpec(memory_space=pltpu.VMEM),) * 4,
        scratch_shapes=[pltpu.SMEM(doc_lengths.shape, jnp.int32)] + [held] * 4
        + [pltpu.SemaphoreType.DMA((5,)), held, pair] + [state] * 7 + [pair, square, square]
        + [pltpu.SemaphoreType.DMA((5, chunks))] * 2,
        compiler_params=pltpu.CompilerParams(
            collective_id=0, has_side_effects=True, vmem_limit_bytes=64946176),
    )(doc_lengths, queries, keys, values, grad_out)
    return pl.pallas_call(
        place,
        out_shape=(out,) * 4,
        in_specs=[pl.BlockSpec(memory_space=pltpu.VMEM)] * 4,
        out_specs=(remote,) * 4,
        scratch_shapes=[pltpu.SemaphoreType.DMA((4,))],
        compiler_params=pltpu.CompilerParams(vmem_limit_bytes=16_000_000),
    )(*results)


def solution(mesh):
    rows = P(("groups", "seq"), None)
    return jax.shard_map(
        functools.partial(per_device, mesh.shape["seq"]),
        mesh=mesh,
        in_specs=(rows, rows, rows, rows, P("groups")),
        out_specs=(rows,) * 4,
        check_vma=False,
    )
```

```python
import functools

import jax
import jax.numpy as jnp
from jax import lax
from jax.experimental import pallas as pl
from jax.experimental.pallas import tpu as pltpu
from jax.sharding import PartitionSpec as P

HD = 128
CHUNK = 2
FORWARD, BACKWARD = 0, 1
MINOR, ACROSS, NEXT, SECOND, CARRY = range(5)
VMEM_BYTES = 67_043_328

F32 = jnp.float32
BF16 = jnp.bfloat16


def dot(a, b, contract=(1, 0)):
    dims = (((contract[0],), (contract[1],)), ((), ()))
    return lax.dot_general(a, b, dims, preferred_element_type=F32)


def pick(flag, x):
    return jnp.where(flag, x.astype(F32), 0.0)


def kernel(n, docs, heads, lengths_hbm, q_hbm, k_hbm, v_hbm, g_hbm, attn_ref, gq_ref, gk_ref, gv_ref,
           lengths, q_ref, k_ref, v_ref, g_ref, load_sems, sg_ref, states, minor_in, sum_out, sum_in,
           total_out, next_in, second_in, carry_out, entering, weights_ref, dweights_ref, send_sems, recv_sems):
    loads = [pltpu.make_async_copy(src, dst, load_sems.at[i]) for i, (src, dst) in enumerate((
        (lengths_hbm, lengths), (g_hbm, g_ref), (q_hbm, q_ref), (k_hbm, k_ref), (v_hbm, v_ref)))]
    for load in loads:
        load.start()
    rows = q_ref.shape[0]
    planes = n // 4
    chunks = heads // CHUNK
    me = lax.axis_index("seq")
    core = lax.rem(me, 2)
    plane = me // 4
    chip = lax.rem(me // 2, 2)
    partner = me + 1 - 2 * core
    across = me + 2 - 4 * chip
    step = 2 * core - 1
    major, minor = 1 - core, core

    def inside(p):
        return (p >= 0) & (p < planes)

    barrier = pltpu.get_barrier_semaphore()

    def greet(device):
        pl.semaphore_signal(barrier, inc=1, device_id={"seq": device},
                            device_id_type=pl.DeviceIdType.MESH)

    greet(partner)
    greet(across)
    for by in (-1, 1):
        @pl.when(inside(plane + by))
        def _():
            greet(me + 4 * by)

    loads[0].wait()
    starts = []
    running = jnp.int32(0)
    for j in range(docs):
        starts.append(running)
        running = running + lengths[j]

    def clear(d, first, last):
        lower = first * rows + d
        upper = (last + 1) * rows + d
        found = jnp.int32(0)
        for s in starts:
            found = found + jnp.where((s >= lower) & (s < upper), 1, 0)
        return found == 0

    own_clear = clear(major, me, me)
    partner_clear = clear(major, partner, partner)
    is_down = chip == core
    down_first = 4 * plane + 2 * core
    up_first = 4 * plane + 2 - 2 * core
    down_clear = clear(major, down_first, down_first + 1)
    up_clear = clear(major, up_first, up_first + 1)
    before_first = 4 * (plane - step)
    before_clear = clear(major, before_first, before_first + 3)
    plane_clear = down_clear & up_clear
    has_before = inside(plane - step)
    has_after = inside(plane + step)
    last = jnp.logical_not(inside(plane + 2 * step))
    merges = has_before & has_after & last & (core == 1)
    relays = has_before & has_after & jnp.logical_not(merges)
    has_second = (has_after | (core == 0)) & inside(plane - 2 * step)
    sends_across = jnp.logical_not(is_down) | has_after
    takes_across = is_down | has_after
    use_next = has_before & (jnp.logical_not(is_down) | up_clear)
    use_second = use_next & before_clear & has_second

    first_row = me * rows
    seq_total = rows * n

    def spans(shape, axis):
        pos = first_row + lax.broadcasted_iota(jnp.int32, shape, axis)
        begin = jnp.zeros(shape, jnp.int32)
        finish = jnp.full(shape, seq_total, jnp.int32)
        for s in starts:
            begin = jnp.where(s <= pos, s, begin)
        for s in reversed(starts):
            finish = jnp.where(s > pos, s, finish)
        return pos, begin, finish

    pos, begin, finish = spans((rows, HD), 0)
    inv_root = 1.0 / jnp.sqrt((pos - begin + 1).astype(F32))
    tail_rows = jnp.where(finish >= first_row + rows, 1.0, 0.0).astype(BF16)
    head_rows = jnp.where(begin <= first_row, 1.0, 0.0).astype(BF16)
    prefix_rows = jnp.where(begin < first_row, 1.0, 0.0).astype(BF16)
    suffix_rows = jnp.where(finish > first_row + rows, 1.0, 0.0).astype(BF16)
    pos_row, begin_row, _ = spans((1, rows), 1)
    pos_square, begin_square, _ = spans((rows, rows), 0)
    same_doc = (begin_square == begin_row) & (pos_row <= pos_square)

    def columns(h):
        return pl.ds(pl.multiple_of(h * HD, HD), HD)

    def copy(kind, i, src, dst, device):
        return pltpu.make_async_remote_copy(
            src_ref=src, dst_ref=dst, send_sem=send_sems.at[kind, i],
            recv_sem=recv_sems.at[kind, i], device_id={"seq": device},
            device_id_type=pl.DeviceIdType.MESH)

    def part(i):
        return pl.ds(i * CHUNK, CHUNK)

    def minor_copy(i):
        return copy(MINOR, i, states.at[minor, part(i)], minor_in.at[part(i)], partner)

    def across_copy(i):
        return copy(ACROSS, i, sum_out.at[part(i)], sum_in.at[part(i)], across)

    def next_copy(i):
        return copy(NEXT, i, total_out.at[part(i)], next_in.at[part(i)], me + 4 * step)

    def second_copy(i):
        return copy(SECOND, i, next_in.at[part(i)], second_in.at[part(i)], me + 4 * step)

    def carry_copy(i):
        return copy(CARRY, i, carry_out.at[part(i)], entering.at[major, part(i)], partner)

    def each(i):
        for j in range(CHUNK):
            h = i * CHUNK + j
            yield h, columns(h)

    def head_states(i):
        for h, at in each(i):
            sg = (g_ref[:, at].astype(F32) * inv_root).astype(BF16)
            sg_ref[:, at] = sg
            states[BACKWARD, h] = dot(q_ref[:, at] * head_rows, sg, (0, 0)).astype(BF16)

    def tail_states(i):
        for h, at in each(i):
            states[FORWARD, h] = dot(k_ref[:, at] * tail_rows, v_ref[:, at], (0, 0)).astype(BF16)

    def scores(i):
        for h, at in each(i):
            w = dot(q_ref[:, at], k_ref[:, at], (1, 1))
            weights_ref[h] = jnp.where(same_doc, w, 0.0).astype(BF16)
            dw = dot(sg_ref[:, at], v_ref[:, at], (1, 1))
            dweights_ref[h] = jnp.where(same_doc, dw, 0.0).astype(BF16)

    def chip_sum(i):
        minor_copy(i).wait_recv()
        for h, _ in each(i):
            sum_out[h] = (states[major, h].astype(F32) + pick(own_clear, minor_in[h])).astype(BF16)

        @pl.when(sends_across)
        def _():
            across_copy(i).start()

    def total(i):
        @pl.when(takes_across)
        def _():
            across_copy(i).wait_recv()

        @pl.when(has_after)
        def _():
            for h, _ in each(i):
                total_out[h] = (pick(is_down | down_clear, sum_out[h])
                                + pick(jnp.logical_not(is_down) | down_clear, sum_in[h])).astype(BF16)

            @pl.when(jnp.logical_not(merges))
            def _():
                next_copy(i).start()

    def relay(i):
        @pl.when(has_before)
        def _():
            next_copy(i).wait_recv()

        @pl.when(merges)
        def _():
            for h, _ in each(i):
                total_out[h] = (total_out[h].astype(F32) + pick(plane_clear, next_in[h])).astype(BF16)
            next_copy(i).start()

    def pass_on(i):
        @pl.when(relays)
        def _():
            second_copy(i).start()

    def enter(i):
        @pl.when(has_second)
        def _():
            second_copy(i).wait_recv()

        for h, _ in each(i):
            carry = pick(is_down, sum_in[h]) + pick(use_next, next_in[h]) + pick(use_second, second_in[h])
            carry_out[h] = carry.astype(BF16)
            entering[major, h] = (minor_in[h].astype(F32) + pick(partner_clear, carry)).astype(BF16)
        carry_copy(i).start()

    def finish_forward(i):
        for h, at in each(i):
            q, sg, state = q_ref[:, at], sg_ref[:, at], entering[FORWARD, h]
            attended = dot(weights_ref[h], v_ref[:, at]) + dot(q * prefix_rows, state)
            attn_ref[:, at] = (attended * inv_root).astype(BF16)
            gq_ref[:, at] = (dot(dweights_ref[h], k_ref[:, at])
                             + dot(sg * prefix_rows, state, (1, 1))).astype(BF16)

    def finish_backward(i):
        for h, at in each(i):
            k, v, state = k_ref[:, at], v_ref[:, at], entering[BACKWARD, h]
            gk_ref[:, at] = (dot(dweights_ref[h], q_ref[:, at], (0, 0))
                             + dot(v * suffix_rows, state, (1, 1))).astype(BF16)
            gv_ref[:, at] = (dot(weights_ref[h], sg_ref[:, at], (0, 0))
                             + dot(k * suffix_rows, state)).astype(BF16)

    def finish_major(i):
        @pl.when(core == 0)
        def _():
            finish_backward(i)

        @pl.when(core == 1)
        def _():
            finish_forward(i)

    def finish_minor(i):
        carry_copy(i).wait_recv()

        @pl.when(core == 0)
        def _():
            finish_forward(i)

        @pl.when(core == 1)
        def _():
            finish_backward(i)

    def at_lag(now, lag, stage, only=True):
        @pl.when((now >= lag) & (now < chunks + lag) & only)
        def _():
            stage(now - lag)

    loads[1].wait()
    loads[2].wait()
    head_states(0)
    peers = jnp.int32(2)
    for by in (-1, 1):
        peers = peers + jnp.where(inside(plane + by), 1, 0)
    pl.semaphore_wait(barrier, peers)

    @pl.when(core == 1)
    def _():
        minor_copy(0).start()

    @pl.loop(1, chunks + 2)
    def _(i):
        @pl.when(i < chunks)
        def _():
            head_states(i)

            @pl.when(core == 1)
            def _():
                minor_copy(i).start()
        at_lag(i, 2, chip_sum, core == 0)

    loads[3].wait()
    loads[4].wait()

    @pl.loop(0, chunks + 4)
    def _(i):
        @pl.when(i < chunks)
        def _():
            tail_states(i)

            @pl.when(core == 0)
            def _():
                minor_copy(i).start()
        at_lag(i, 0, scores, core == 1)
        at_lag(i, 4, chip_sum, core == 1)

    enter_lag = jnp.where(has_second, 5, 3)
    minor_lag = jnp.where(core == 0, 7, 5)

    @pl.loop(0, chunks + 7)
    def _(i):
        at_lag(i, 0, scores, core == 0)
        at_lag(i, 0, total)
        at_lag(i, 2, relay)
        at_lag(i, 2, pass_on)
        at_lag(i, enter_lag, enter)
        at_lag(i, enter_lag, finish_major)
        at_lag(i, minor_lag, finish_minor)

    @pl.loop(0, chunks)
    def _(i):
        minor_copy(i).wait_send()
        carry_copy(i).wait_send()

        @pl.when(sends_across)
        def _():
            across_copy(i).wait_send()

        @pl.when(has_after)
        def _():
            next_copy(i).wait_send()

        @pl.when(relays)
        def _():
            second_copy(i).wait_send()


def place(*refs):
    sources, targets, sems = refs[:4], refs[4:8], refs[8]
    moves = [pltpu.make_async_copy(src, dst, sems.at[i]) for i, (src, dst) in enumerate(zip(sources, targets))]
    for move in moves:
        move.start()
    for move in moves:
        move.wait()


def per_device(n, queries, keys, values, grad_out, doc_lengths):
    rows, width = queries.shape
    heads = width // HD
    chunks = heads // CHUNK
    remote = pl.BlockSpec(memory_space=pltpu.HBM)
    local = pl.BlockSpec(memory_space=pltpu.VMEM)
    held = pltpu.VMEM((rows, width), BF16)
    state = pltpu.VMEM((heads, HD, HD), BF16)
    pair = pltpu.VMEM((2, heads, HD, HD), BF16)
    square = pltpu.VMEM((heads, rows, rows), BF16)
    out = jax.ShapeDtypeStruct((rows, width), BF16)
    outputs_bytes = 4 * rows * width * 2
    results = pl.pallas_call(
        functools.partial(kernel, n, doc_lengths.shape[0], heads),
        out_shape=(held,) * 4,
        in_specs=[remote] * 5,
        out_specs=(local,) * 4,
        scratch_shapes=[pltpu.SMEM(doc_lengths.shape, jnp.int32)] + [held] * 4
        + [pltpu.SemaphoreType.DMA((5,)), held, pair] + [state] * 7 + [pair, square, square]
        + [pltpu.SemaphoreType.DMA((5, chunks))] * 2,
        compiler_params=pltpu.CompilerParams(
            collective_id=0, has_side_effects=True, vmem_limit_bytes=VMEM_BYTES - outputs_bytes),
    )(doc_lengths, queries, keys, values, grad_out)
    return pl.pallas_call(
        place,
        out_shape=(out,) * 4,
        in_specs=[local] * 4,
        out_specs=(remote,) * 4,
        scratch_shapes=[pltpu.SemaphoreType.DMA((4,))],
        compiler_params=pltpu.CompilerParams(vmem_limit_bytes=16_000_000),
    )(*results)


def solution(mesh):
    rows = P(("groups", "seq"), None)
    return jax.shard_map(
        functools.partial(per_device, mesh.shape["seq"]),
        mesh=mesh,
        in_specs=(rows, rows, rows, rows, P("groups")),
        out_specs=(rows,) * 4,
        check_vma=False,
    )
```
